512 devices in a mesh: expert: 64 (over x, z), dp: 4 (over y), test: 2 (over core).
Axes of the slice: x: 4, y: 4, z: 16, core: 2. Of those that a mesh axis runs over, the one named last changes fastest.
Arguments:
- tokens: bfloat16 [16384, 3584], P(('expert', 'dp'), 'test'), may hold values from -6 to 6
- out_grad: bfloat16 [16384, 3584], P(('expert', 'dp'), 'test'), may hold values from -6 to 6
- route_ids: int32 [16384, 8], P(('expert', 'dp')), may hold values from 0 to 255, as said below
- route_slots: int32 [16384, 8], P(('expert', 'dp')), may hold values from -1 to 1, as said below
- route_weight: bfloat16 [16384, 8], P(('expert', 'dp')), may hold values from 0.19921875 to 1
- w_gate: bfloat16 [64, 3584, 1024], P('expert', None, ('dp', 'test')), may hold values from -0.09375 to 0.09375
- w_up: bfloat16 [64, 3584, 1024], P('expert', None, ('dp', 'test')), may hold values from -0.09375 to 0.09375
- w_down: bfloat16 [64, 1024, 3584], P('expert', ('dp', 'test')), may hold values from -0.1875 to 0.1875
- proj_hidden: bfloat16 [64, 64, 1024], P('expert', None, ('dp', 'test')), may hold values from -0.1875 to 0.1875
- proj_grad: bfloat16 [64, 64, 3584], P('expert'), may hold values from -0.09375 to 0.09375
- test_feats: bfloat16 [64, 256, 4096], P('expert', 'test'), may hold values from -0.09375 to 0.09375
Outputs:
- in_grad: bfloat16 [16384, 3584], P(('expert', 'dp'), 'test')
- scores: float32 [16384, 256], P(('expert', 'dp'), 'test')
The draws below stay inside these ranges and needn't reach their ends.
Inputs may be any that keep to these rules, and one draw needn't show every extreme that they name: `route_ids`: each row names 8 different experts. `route_slots`: A route's slot is -1 exactly when its expert is 64 or more, or when 2 earlier tokens of the same aligned block of 64 rows already take that expert; otherwise it is the number of earlier tokens of that block routed to that expert.
All inputs are finite; a program needn't handle non-finite values.
Results may differ from the reference program's by a relative error of at most 0.0065.
Values may be sent and summed in bfloat16 or wider, within the bound.
A program may use at most 64 MiB of HBM per device.

```python
import jax
import jax.numpy as jnp
from jax import lax

D = 3584
FF = 1024
ROUTED = 256
TOPK = 8
PROJ = 64
TOK_DEV = 64
NTEST = 256
CAP = 2
EXPERTS = 64
TOKENS = 16384
N_DP = 4
N_TEST = 2


def route_table(key):
    base_key = jax.random.fold_in(key, 11)
    key_pop, key_noise, key_pick = jax.random.split(base_key, 3)
    blocks = TOKENS // TOK_DEV
    popularity = jax.random.randint(key_pop, (ROUTED,), 0, 3).astype(jnp.int32)
    noise_bits = jax.random.randint(key_noise, (TOKENS, ROUTED), 0, 1 << 20).astype(jnp.int32)
    picked = jax.random.randint(key_pick, (blocks,), 0, EXPERTS).astype(jnp.int32)
    row_ids = jnp.arange(TOKENS, dtype=jnp.int32)
    local_row = row_ids % TOK_DEV
    column = jnp.arange(ROUTED, dtype=jnp.int32)
    forced = (local_row[:, None] < CAP) & (column[None, :] == picked[row_ids // TOK_DEV][:, None])
    priority = (noise_bits + popularity[None, :] * (1 << 18)) * ROUTED + column[None, :] + forced.astype(jnp.int32) * (1 << 30)
    chosen_ids = lax.top_k(priority, TOPK)[1].astype(jnp.int32)
    chosen = jnp.sum((chosen_ids[:, :, None] == column[None, None, :]).astype(jnp.int32), axis=1)
    earlier = jnp.cumsum(chosen.reshape(blocks, TOK_DEV, ROUTED), axis=1).reshape(TOKENS, ROUTED) - chosen
    order_rank = jnp.take_along_axis(earlier, chosen_ids, axis=1)
    live_mask = (chosen_ids < EXPERTS) & (order_rank < CAP)
    slot_ids = jnp.where(live_mask, order_rank, -1).astype(jnp.int32)
    return (chosen_ids, slot_ids)


def draw_route_ids(key, part):
    return route_table(key)[0]


def draw_route_slots(key, part):
    return route_table(key)[1]


def block_scale(own_key, dims, cuts, low, largest):
    def one(position, parts):
        steps = jax.random.uniform(jax.random.fold_in(jax.random.fold_in(own_key, 6), position), (parts,), jnp.float32, low / len(cuts), largest / len(cuts))
        return jnp.repeat(jnp.exp(steps), dims[position] // parts).reshape((-1,) + (1,) * (len(dims) - position - 1))

    factor_of = one(*cuts[0])
    for cut in cuts[1:]:
        factor_of = factor_of * one(*cut)
    return factor_of


def bell_draw(rng, shape, scale, limit, cuts=(), kind=jnp.bfloat16):
    loudness = block_scale(rng, shape, cuts, -0.22, 0.18) if cuts else 1.0
    result = jax.random.normal(rng, shape, jnp.float32) * scale * loudness
    return jnp.minimum(jnp.maximum(result, -limit), limit).astype(kind)


def setup_inputs(seed: int = 0) -> dict:
    streams_of = jax.random.split(jax.random.key(seed), 12)
    return {
        "tokens": bell_draw(streams_of[0], (TOKENS, D), 1.0, 6.0, ((0, 256), (1, 2))),
        "out_grad": bell_draw(streams_of[1], (TOKENS, D), 1.0, 6.0, ((0, 256), (1, 2))),
        "route_ids": draw_route_ids(jax.random.fold_in(streams_of[11], 71), 0),
        "route_slots": draw_route_slots(jax.random.fold_in(streams_of[11], 71), 0),
        "route_weight": jnp.clip(0.19921875 + 0.80078125 * jax.random.uniform(streams_of[4], (TOKENS, TOPK), jnp.float32) ** block_scale(streams_of[4], (TOKENS, TOPK), ((0, 256),), -0.2, 0.2), 0.19921875, 1.0).astype(jnp.bfloat16),
        "w_gate": bell_draw(streams_of[5], (EXPERTS, D, FF), D ** -0.5, 0.09375, ((0, 64), (2, 8))),
        "w_up": bell_draw(streams_of[6], (EXPERTS, D, FF), D ** -0.5, 0.09375, ((0, 64), (2, 8))),
        "w_down": bell_draw(streams_of[7], (EXPERTS, FF, D), FF ** -0.5, 0.1875, ((0, 64), (1, 8))),
        "proj_hidden": bell_draw(streams_of[8], (EXPERTS, PROJ, FF), FF ** -0.5, 0.1875, ((0, 64), (2, 8))),
        "proj_grad": bell_draw(streams_of[9], (EXPERTS, PROJ, D), D ** -0.5, 0.09375, ((0, 64),)),
        "test_feats": bell_draw(streams_of[10], (EXPERTS, NTEST, PROJ * PROJ), (PROJ * PROJ) ** -0.5, 0.09375, ((0, 64), (1, 2))),
    }


def reference(tokens, out_grad, route_ids, route_slots, route_weight, w_gate, w_up, w_down, proj_hidden, proj_grad, test_feats):
    blocks = TOKENS // TOK_DEV
    slot_rows = blocks * CAP
    row_ids = jnp.arange(TOKENS, dtype=jnp.int32)
    live_mask = (route_slots >= 0) & (route_ids < EXPERTS)
    where_to = jnp.where(live_mask, route_ids * slot_rows + (row_ids // TOK_DEV)[:, None] * CAP + route_slots, EXPERTS * slot_rows).astype(jnp.int32)
    owners = jnp.broadcast_to(row_ids[:, None], where_to.shape).astype(jnp.int32)
    holder = jnp.full((EXPERTS * slot_rows,), TOKENS, jnp.int32).at[where_to.reshape(-1)].set(owners.reshape(-1), mode="drop")
    route_scale = jnp.zeros((EXPERTS * slot_rows,), jnp.float32).at[where_to.reshape(-1)].set(route_weight.astype(jnp.float32).reshape(-1), mode="drop")
    holder = holder.reshape(EXPERTS, slot_rows)
    route_scale = route_scale.reshape(EXPERTS, slot_rows)
    blocks_ff = N_DP * N_TEST
    ff_block = FF // blocks_ff

    def one_expert(totals, per_expert):
        grad_sum, score_sum = totals
        slot_owner, factor, gate_w, up_w, down_w, hid_proj, grad_proj, test_rows = per_expert
        valid_rows = slot_owner < TOKENS
        safe_index = jnp.minimum(slot_owner, TOKENS - 1).astype(jnp.int32)
        expert_in = jnp.where(valid_rows[:, None], tokens[safe_index], jnp.zeros((), tokens.dtype))
        expert_grad = (factor[:, None] * out_grad[safe_index].astype(jnp.float32)).astype(jnp.bfloat16)
        gate_pre = jnp.dot(expert_in, gate_w, preferred_element_type=jnp.float32)
        up_pre = jnp.dot(expert_in, up_w, preferred_element_type=jnp.float32)
        sigmoid_gate = jax.nn.sigmoid(gate_pre)
        act_gate = gate_pre * sigmoid_gate
        hidden = (act_gate * up_pre).astype(jnp.bfloat16)
        hidden_proj = jnp.dot(hidden, hid_proj.T, preferred_element_type=jnp.float32)
        grad_vec = jnp.dot(expert_grad, grad_proj.T, preferred_element_type=jnp.float32)
        hidden_grad = jnp.dot(expert_grad, down_w.T, preferred_element_type=jnp.float32)
        up_grad = (hidden_grad * act_gate).astype(jnp.bfloat16)
        gate_grad = (hidden_grad * up_pre * sigmoid_gate * (1.0 + gate_pre * (1.0 - sigmoid_gate))).astype(jnp.bfloat16)
        row_total = gate_grad.shape[0]
        pieces = jnp.einsum("rbf,dbf->brd", gate_grad.astype(jnp.float32).reshape(row_total, blocks_ff, ff_block), gate_w.astype(jnp.float32).reshape(D, blocks_ff, ff_block))
        pieces = pieces + jnp.einsum("rbf,dbf->brd", up_grad.astype(jnp.float32).reshape(row_total, blocks_ff, ff_block), up_w.astype(jnp.float32).reshape(D, blocks_ff, ff_block))
        pieces = lax.optimization_barrier(pieces.astype(jnp.bfloat16)).astype(jnp.float32)
        route_grad = jnp.sum(pieces, axis=0)
        feature = (hidden_proj[:, :, None] * grad_vec[:, None, :]).reshape(row_total, PROJ * PROJ).astype(jnp.bfloat16)
        route_score = jnp.dot(feature, test_rows.T, preferred_element_type=jnp.float32).astype(jnp.bfloat16)
        grad_sum = grad_sum.at[slot_owner].add(route_grad, mode="drop")
        score_sum = score_sum.at[slot_owner].add(route_score.astype(jnp.float32), mode="drop")
        return (grad_sum, score_sum), None

    initial = (jnp.zeros((TOKENS, D), jnp.float32), jnp.zeros((TOKENS, NTEST), jnp.float32))
    (grad_sum, score_sum), _ = lax.scan(one_expert, initial, (holder, route_scale, w_gate, w_up, w_down, proj_hidden, proj_grad, test_feats))
    return grad_sum.astype(jnp.bfloat16), score_sum
```

```python
import jax
import jax.numpy as jnp
from jax import lax
from jax.sharding import PartitionSpec as P

CAP = 2


def pick_tables(ids_in, slots_in, weights_in, experts):
    live_mask = (slots_in >= 0) & (ids_in < experts)
    slot_code = jnp.where(live_mask, ids_in * CAP + slots_in, -1)
    columns = jnp.arange(experts * CAP, dtype=jnp.int32)
    matches = slot_code[:, :, None] == columns[None, None, :]
    picks = jnp.sum(matches.astype(jnp.float32), axis=1)
    weighted = jnp.sum(jnp.where(matches, weights_in.astype(jnp.float32)[:, :, None], 0.0), axis=1)
    return (picks.astype(jnp.bfloat16), weighted.astype(jnp.bfloat16))


def dot(a, b, ca, cb):
    return lax.dot_general(a, b, (((ca,), (cb,)), ((), ())), preferred_element_type=jnp.float32)


def on_device(
    tokens,
    out_grad,
    route_ids,
    route_slots,
    route_weight,
    w_gate,
    w_up,
    w_down,
    proj_hidden,
    proj_grad,
    test_feats,
):
    experts = lax.axis_size("expert")
    groups = lax.axis_size("dp")
    halves = lax.axis_size("test")
    half = tokens.shape[1]
    slots = experts * CAP
    pick, weighted = pick_tables(route_ids, route_slots, route_weight, experts)
    in_buf = dot(pick, tokens, 0, 0).astype(jnp.bfloat16)
    grad_buf = dot(weighted, out_grad, 0, 0).astype(jnp.bfloat16)

    def exchange(rows):
        width = rows.shape[1]
        moved = lax.all_to_all(
            rows.reshape(experts, CAP, width), "expert", split_axis=0, concat_axis=0, tiled=True
        )
        return moved.reshape(slots, width)

    def spread(rows):
        full = lax.all_gather(rows, ("dp", "test"), axis=0, tiled=True)
        full = full.reshape(groups, halves, slots, half)
        return [full[:, h].reshape(groups * slots, half) for h in range(halves)]

    mine_in = exchange(in_buf)
    ins = spread(mine_in)
    mine_grad = exchange(grad_buf)
    grads = spread(mine_grad)

    gate_w, up_w, down_w = w_gate[0], w_up[0], w_down[0]

    def cut(arr, h, axis):
        return lax.slice_in_dim(arr, h * half, (h + 1) * half, axis=axis)

    gate_pre = sum(dot(ins[h], cut(gate_w, h, 0), 1, 0) for h in range(halves))
    up_pre = sum(dot(ins[h], cut(up_w, h, 0), 1, 0) for h in range(halves))
    sig = jax.nn.sigmoid(gate_pre)
    act = gate_pre * sig
    hidden = (act * up_pre).astype(jnp.bfloat16)
    proj_part = dot(hidden, proj_hidden[0], 1, 1)
    hid_grad = sum(dot(grads[h], cut(down_w, h, 1), 1, 1) for h in range(halves))
    up_grad = (hid_grad * act).astype(jnp.bfloat16)
    gate_grad = (hid_grad * up_pre * sig * (1.0 + gate_pre * (1.0 - sig))).astype(jnp.bfloat16)
    parts = [
        (dot(gate_grad, cut(gate_w, h, 0), 1, 1) + dot(up_grad, cut(up_w, h, 0), 1, 1)).astype(
            jnp.bfloat16
        )
        for h in range(halves)
    ]
    parts = jnp.stack([p.reshape(groups, slots, half) for p in parts], axis=1)
    mine_back = lax.psum_scatter(
        parts.reshape(groups * halves * slots, half), ("dp", "test"), scatter_dimension=0, tiled=True
    )
    back = exchange(mine_back.astype(jnp.bfloat16))
    in_grad = dot(pick, back, 1, 0).astype(jnp.bfloat16)

    hidden_vec = lax.psum(proj_part, ("dp", "test"))
    me = lax.axis_index("dp")
    hid_mine = lax.dynamic_slice_in_dim(hidden_vec, me * slots, slots, 0)
    grad_mine = sum(
        dot(lax.dynamic_slice_in_dim(grads[h], me * slots, slots, 0), cut(proj_grad[0], h, 1), 1, 1)
        for h in range(halves)
    )
    feature = (hid_mine[:, :, None] * grad_mine[:, None, :]).reshape(slots, -1).astype(jnp.bfloat16)
    score = dot(feature, test_feats[0], 1, 1).astype(jnp.bfloat16)
    scores = dot(pick, exchange(score), 1, 0)
    return (in_grad, scores)


def solution(mesh):
    placed = (
        P(("expert", "dp"), "test"),
        P(("expert", "dp"), "test"),
        P(("expert", "dp"), None),
        P(("expert", "dp"), None),
        P(("expert", "dp"), None),
        P("expert", None, ("dp", "test")),
        P("expert", None, ("dp", "test")),
        P("expert", ("dp", "test"), None),
        P("expert", None, ("dp", "test")),
        P("expert", None, None),
        P("expert", "test", None),
    )
    return jax.shard_map(
        on_device,
        mesh=mesh,
        in_specs=placed,
        out_specs=(P(("expert", "dp"), "test"), P(("expert", "dp"), "test")),
        check_vma=False,
    )
```
